32 devices in a mesh: tile: 4 (over x, core), row: 8 (over z, y).
Axes of the slice: x: 2, y: 2, z: 4, core: 2. Of those that a mesh axis runs over, the one named last changes fastest.
Arguments:
- factor_u: bfloat16 [3072, 96, 512], P(('tile', 'row')), may hold values from -0.625 to 0.625
- factor_v: bfloat16 [3072, 96, 512], P(('tile', 'row')), may hold values from -0.25 to 0.25
- tile_ranks: int32 [3072], P(('tile', 'row')), may hold values from 16 to 96
- tile_rows: int32 [3072, 1], P(('tile', 'row')), may hold values from 0 to 31; in each aligned block of 96 rows (0 to 95, 96 to 191, ...) at most 3 rows name the same one
- tile_cols: int32 [3072], P(('tile', 'row')), may hold values from 0 to 31
- cluster_home: int32 [32], replicated, may hold values from 0 to 31, each once
- quad_weights: float32 [32, 512], replicated, may hold values from 0.3 to 3
- test_matrix: bfloat16 [512, 128], replicated, may hold values from -6 to 6
- near_sketch: bfloat16 [32, 512, 128], P(('tile', 'row')), may hold values from -24 to 24
Outputs:
- couplings: float32 [3072, 128, 128], P(('tile', 'row'))
The draws below stay inside these ranges and needn't reach their ends.
Inputs may be any that keep to these rules, and one draw needn't show every extreme that they name: `tile_rows`: among the 96 tiles of one device no row cluster appears more than 3 times, and in some devices one appears exactly 3 times. `cluster_home`: each of 0 to 31 appears once; the home index is the device's index along tile+row.
All inputs are finite; a program needn't handle non-finite values.
Results may differ from the reference program's by a relative error of at most 0.0074.
Values may be sent and summed in bfloat16 or wider, within the bound.
A program may use at most 192 MiB of HBM per device.

```python
import math
import jax
import jax.numpy as jnp
import numpy as np
from jax import lax

NODES = 512
BASIS = 128
RMAX = 96
RMIN = 16
TILE_DEV = 96
CLUSTERS = 32
MOST = 3
TILES = 3072


def touch_ends(result, key, least, high):
    place = [jax.random.randint(jax.random.fold_in(key, axis), (), 0, length) for axis, length in enumerate(result.shape)]
    main_axis = result.shape.index(max(result.shape))
    next_to = place[:main_axis] + [(place[main_axis] + 1) % result.shape[main_axis]] + place[main_axis + 1:]
    return result.at[tuple(place)].set(least).at[tuple(next_to)].set(high)


def block_scale(rng, extent, cuts, smallest, high):
    gain, own = 1.0, jax.random.fold_in(rng, 6)
    for dim, blocks in cuts:
        draws = jnp.exp(jax.random.uniform(jax.random.fold_in(own, dim), (blocks,), jnp.float32, smallest / len(cuts), high / len(cuts)))
        gain = gain * jnp.repeat(draws, extent[dim] // blocks).reshape([-1 if axis == dim else 1 for axis in range(len(extent))])
    return gain


def routed_block(rng, own, number, rows, number_of, top, reach, lean):
    ranking = jax.random.permutation(rng, number_of)
    heavy_load, usual = portions_of(number_of, rows * top, reach, lean, True), portions_of(number_of, rows * top, reach, lean, False)
    places = jnp.arange(number_of)

    def named(lengths, offset_by):
        used = int((lengths > 0).sum())
        fixed = max(1, used // 4)
        passed = fixed + (places - fixed + offset_by * (used - fixed)) % max(1, number_of - fixed)
        return jnp.zeros((number_of,), jnp.int32).at[ranking[jnp.where(places < fixed, places, passed)]].set(jnp.asarray(lengths, jnp.int32))

    lengths = jnp.where(number % 4 == 0, named(heavy_load, number // 4), named(usual, number - number // 4 - 1))
    mixed = jax.random.permutation(jax.random.fold_in(own, 3), number_of)
    donor, receiver = mixed[0:number_of // 2 * 2:2], mixed[1:number_of // 2 * 2:2]
    slack = jnp.minimum(lengths[donor] - 1, reach - lengths[receiver]) // 2
    slack = jnp.where((donor == ranking[0]) | (receiver == ranking[0]) | (lengths[receiver] == 0), 0, jnp.maximum(slack, 0))
    passed = jax.random.randint(jax.random.fold_in(own, 4), (number_of // 2,), 0, 1 << 20) % (slack + 1)
    lengths = lengths.at[donor].add(-passed).at[receiver].add(passed)
    members = jnp.searchsorted(jnp.cumsum(lengths), jnp.arange(rows * top), side="right").astype(jnp.int32)
    table = members.reshape(top, rows).T
    table = table[jax.random.permutation(jax.random.fold_in(own, 1), rows)]
    offset_by = jax.random.randint(jax.random.fold_in(own, 2), (rows, 1), 0, top)
    return jnp.take_along_axis(table, (jnp.arange(top)[None, :] + offset_by) % top, axis=1)


def portions_of(number_of, total, limit, lean, full):
    weights = [(1 << 20) // math.isqrt(rank ** lean) + 1 for rank in range(1, number_of + 1)]
    largest = limit if full else min(limit, max(-(-total // number_of), total * weights[0] // sum(weights)))
    least = 1 if total - largest >= number_of - 1 else 0
    counts, rest = [largest] + [least] * (number_of - 1), total - largest - least * (number_of - 1)
    while rest > 0:
        movable = [i for i in range(1, number_of) if counts[i] < largest] or [i for i in range(1, number_of) if counts[i] < limit]
        pool, left = sum([weights[i] for i in movable]), rest
        for i in movable:
            extra = min(limit - counts[i], max(1, left * weights[i] // pool), rest)
            counts[i] = counts[i] + extra
            rest = rest - extra
    return np.array(counts)


def normal_values(own_key, dims, scale, most, pieces=(), kind=jnp.bfloat16):
    loudness = block_scale(own_key, dims, pieces, -0.22, 0.18) if pieces else 1.0
    entries = jax.random.normal(own_key, dims, jnp.float32) * scale * loudness
    return jnp.minimum(jnp.maximum(entries, -most), most).astype(kind)


def setup_inputs(seed: int = 0) -> dict:
    key_list = jax.random.split(jax.random.key(seed), 10)
    factor_u = normal_values(key_list[0], (TILES, RMAX, NODES), RMAX ** -0.5, 0.625, ((0, 32),))
    factor_v = normal_values(key_list[1], (TILES, RMAX, NODES), NODES ** -0.5, 0.25, ((0, 32),))
    tile_ranks = touch_ends(jax.random.randint(key_list[2], (TILES,), RMIN, RMAX + 1), jax.random.fold_in(key_list[2], 1), RMIN, RMAX).astype(jnp.int32)
    tile_rows_keys = jax.random.split(jax.random.fold_in(key_list[3], 1), TILES // TILE_DEV)
    tile_rows_turns = jax.random.permutation(jax.random.fold_in(key_list[3], 3), TILES // TILE_DEV)
    tile_rows = jax.vmap(lambda own, number: routed_block(jax.random.fold_in(key_list[3], 2), own, number, TILE_DEV, CLUSTERS, 1, MOST, 2))(tile_rows_keys, tile_rows_turns).reshape((TILES, 1))
    tile_cols = touch_ends(jax.random.randint(key_list[4], (TILES,), 0, CLUSTERS), jax.random.fold_in(key_list[4], 1), 0, CLUSTERS - 1).astype(jnp.int32)
    cluster_home = jax.random.permutation(key_list[5], CLUSTERS).astype(jnp.int32)
    quad_weights = jnp.clip(jnp.exp(jax.random.uniform(key_list[6], (CLUSTERS, NODES), jnp.float32, math.log(0.3), math.log(3.0))), 0.3, 3.0)
    test_matrix = normal_values(key_list[7], (NODES, BASIS), 1.0, 6.0)
    near_sketch = normal_values(key_list[8], (CLUSTERS, NODES, BASIS), 4.0, 24.0, ((0, 32),))
    return dict(factor_u=factor_u, factor_v=factor_v, tile_ranks=tile_ranks, tile_rows=tile_rows, tile_cols=tile_cols, cluster_home=cluster_home, quad_weights=quad_weights, test_matrix=test_matrix, near_sketch=near_sketch)


def make_parts(factor_u, factor_v, ranks, columns, quad_weights, test_matrix):
    live_cols = jnp.arange(RMAX, dtype=jnp.int32)[None, :] < ranks[:, None]
    masked_u = jnp.where(live_cols[:, :, None], factor_u, jnp.zeros((), jnp.bfloat16))
    weighted_v = (factor_v.astype(jnp.float32) * quad_weights[columns][:, None, :]).astype(jnp.bfloat16)
    sketch = jnp.dot(weighted_v.reshape(-1, NODES).astype(jnp.float32), test_matrix.astype(jnp.float32), preferred_element_type=jnp.float32)
    sketch = sketch.astype(jnp.bfloat16).reshape(-1, RMAX, BASIS)
    return (masked_u, sketch)

def reference(factor_u, factor_v, tile_ranks, tile_rows, tile_cols, cluster_home, quad_weights, test_matrix, near_sketch):
    blocks = TILES // TILE_DEV
    home_index = cluster_home[tile_rows[:, 0]]
    grouped = (factor_u.reshape(blocks, TILE_DEV, RMAX, NODES), factor_v.reshape(blocks, TILE_DEV, RMAX, NODES), tile_ranks.reshape(blocks, TILE_DEV), tile_cols.reshape(blocks, TILE_DEV), home_index.reshape(blocks, TILE_DEV))

    def accumulate(total, group):
        block_u, block_v, ranks, columns, homes = group
        masked_u, sketch = make_parts(block_u, block_v, ranks, columns, quad_weights, test_matrix)
        terms = jnp.einsum('tkn,tkc->tnc', masked_u.astype(jnp.float32), sketch.astype(jnp.float32))
        return (total.at[homes].add(terms), None)
    far_part, _ = lax.scan(accumulate, jnp.zeros((CLUSTERS, NODES, BASIS), jnp.float32), grouped)
    sketched = near_sketch.astype(jnp.float32) + far_part
    gram_matrix = jnp.einsum('hnc,hne->hce', sketched, sketched, precision=lax.Precision.HIGHEST)
    lower_factor = jnp.linalg.cholesky(gram_matrix)
    basis_rows = lax.linalg.triangular_solve(lower_factor, jnp.swapaxes(sketched, 1, 2), left_side=True, lower=True)
    basis_half = basis_rows.astype(jnp.bfloat16)

    def project(group):
        block_u, block_v, ranks, columns, homes = group
        masked_u, sketch = make_parts(block_u, block_v, ranks, columns, quad_weights, test_matrix)
        chosen = basis_half[homes].astype(jnp.float32)
        own_proj = jnp.einsum('tkn,tcn->tkc', masked_u.astype(jnp.float32), chosen).astype(jnp.bfloat16)
        return jnp.einsum('tkc,tke->tce', own_proj.astype(jnp.float32), sketch.astype(jnp.float32))
    couplings = lax.map(project, grouped)
    return couplings.reshape(TILES, BASIS, BASIS)
```

```python
import functools

import jax
import jax.numpy as jnp
from jax import lax
from jax.experimental import pallas as pl
from jax.experimental.pallas import tpu as pltpu
from jax.sharding import PartitionSpec as P

MESH = pl.DeviceIdType.MESH
DEPTH = 4
VMEM = pl.BlockSpec(memory_space=pltpu.VMEM)


def grid_of(sizes):
    return {"x": sizes[0] // 2, "z": DEPTH, "y": sizes[1] // DEPTH}


def where_am_i(sizes):
    dims = grid_of(sizes)
    tile, row = lax.axis_index("tile"), lax.axis_index("row")
    here = {"x": tile // 2, "z": row // dims["y"], "y": row % dims["y"]}
    return dims, here, tile % 2


def device(dims, here, core, **moved):
    at = dict(here, **moved)
    return (at["x"] * 2 + core, at["z"] * dims["y"] + at["y"])


def greet(dims, here, core):
    barrier = pltpu.get_barrier_semaphore()
    pl.semaphore_signal(barrier, inc=1, device_id=device(dims, here, 1 - core), device_id_type=MESH)
    for axis, extent in dims.items():
        place = here[axis]

        @pl.when(place > 0)
        def _():
            pl.semaphore_signal(barrier, inc=1, device_id=device(dims, here, core, **{axis: place - 1}), device_id_type=MESH)

        @pl.when(place < extent - 1)
        def _():
            pl.semaphore_signal(barrier, inc=1, device_id=device(dims, here, core, **{axis: place + 1}), device_id_type=MESH)

    heard = 1
    for axis, extent in dims.items():
        heard = heard + jnp.where(here[axis] > 0, 1, 0) + jnp.where(here[axis] < extent - 1, 1, 0)
    pl.semaphore_wait(barrier, heard)


PARTS = ((0, 48, ("z", "x", "y")), (48, 48, ("x", "y", "z")), (96, 32, ("y", "z", "x")))
AXES = ("x", "z", "y")


def view(here, done, fixed, start, rows, core=None):
    index = []
    for axis in AXES:
        if axis in fixed:
            index.append(fixed[axis])
        elif axis in done:
            index.append(here[axis])
        else:
            index.append(slice(None))
        if axis == "x" and core is not None:
            index.append(core)
    return tuple(index) + (pl.ds(start, rows), slice(None))


def reduce_kernel(sizes, part_ref, far_ref, held, *scratch):
    boxes, (core_send, core_recv, send_sem, recv_sem) = scratch[:-4], scratch[-4:]
    dims, here, core = where_am_i(sizes)
    greet(dims, here, core)
    sems = {}

    def sem_of(*key):
        return sems.setdefault(key, len(sems))

    box_of = {}
    for number, (_, _, order) in enumerate(PARTS):
        for phase in range(3):
            for way in range(2):
                box_of[number, phase, way] = boxes[len(box_of)]

    core_copies = {}
    for number, (start, rows, _) in enumerate(PARTS):
        copies = []
        for x in range(dims["x"]):
            slot = sem_of("core", number, x)
            copy = pltpu.make_async_remote_copy(
                src_ref=part_ref.at[x, 1 - core, :, :, pl.ds(start, rows), :],
                dst_ref=held.at[x, :, :, pl.ds(start, rows), :],
                send_sem=core_send.at[slot],
                recv_sem=core_recv.at[slot],
                device_id=device(dims, here, 1 - core),
                device_id_type=MESH,
            )
            copy.start()
            copies.append(copy)
        core_copies[number] = copies

    zs, ys = dims["z"], dims["y"]

    def core_sum(number):
        start, rows, _ = PARTS[number]
        for x, copy in enumerate(core_copies[number]):
            copy.wait_recv()

            def add(i, carry):
                z, y = i // ys, i % ys
                own = part_ref[x, core, z, y, pl.ds(start, rows), :].astype(jnp.float32)
                got = held[x, z, y, pl.ds(start, rows), :].astype(jnp.float32)
                held[x, z, y, pl.ds(start, rows), :] = (own + got).astype(jnp.bfloat16)
                return carry

            lax.fori_loop(0, zs * ys, add, 0)

    def rest_of(order, phase):
        left = [axis for axis in AXES if axis not in order[: phase + 1]]
        count = 1
        for axis in left:
            count *= dims[axis]
        return left, count

    def each(order, phase, body):
        left, count = rest_of(order, phase)

        def step(i, carry):
            at, rem = {}, i
            for axis in reversed(left):
                at[axis] = rem % dims[axis]
                rem = rem // dims[axis]
            body(at, tuple(at[axis] for axis in left))
            return carry

        if count == 1:
            step(0, 0)
        else:
            lax.fori_loop(0, count, step, 0)

    def link(number, phase, way, goal):
        start, rows, order = PARTS[number]
        axis = order[phase]
        slot = (number * 3 + phase) * 8 + way * 4 + goal
        to = here[axis] + 1 if way == 0 else here[axis] - 1
        return pltpu.make_async_remote_copy(
            src_ref=held.at[view(here, order[:phase], {axis: goal}, start, rows)],
            dst_ref=box_of[number, phase, way].at[goal],
            send_sem=send_sem.at[slot],
            recv_sem=recv_sem.at[slot],
            device_id=device(dims, here, core, **{axis: to}),
            device_id_type=MESH,
        )

    def runs(way, axis, goal):
        place, extent = here[axis], dims[axis]
        sends = place < goal if way == 0 else place > goal
        relays = place > 0 if way == 0 else place < extent - 1
        return sends, relays

    def goals_of(axis):
        extent = dims[axis]
        for i in range(1, extent):
            yield 0, extent - i
            yield 1, i - 1

    def chain(number, phase):
        start, rows, order = PARTS[number]
        axis = order[phase]
        for way, goal in goals_of(axis):
            sends, relays = runs(way, axis, goal)

            @pl.when(sends)
            def _():
                @pl.when(relays)
                def _():
                    link(number, phase, way, goal).wait_recv()

                    def body(at, rest):
                        index = view(here, order[:phase], dict(at, **{axis: goal}), start, rows)
                        total = held[index].astype(jnp.float32) + box_of[number, phase, way][(goal,) + rest].astype(jnp.float32)
                        held[index] = total.astype(jnp.bfloat16)

                    each(order, phase, body)

                link(number, phase, way, goal).start()

    def finish(number, phase):
        start, rows, order = PARTS[number]
        axis = order[phase]
        place, extent = here[axis], dims[axis]

        def total_up(ways):
            for way in ways:
                link(number, phase, way, place).wait_recv()

            def body(at, rest):
                index = view(here, order[:phase], dict(at, **{axis: place}), start, rows)
                total = held[index].astype(jnp.float32)
                for way in ways:
                    total = total + box_of[number, phase, way][(place,) + rest].astype(jnp.float32)
                if phase == 2:
                    far_ref[pl.ds(start, rows), :] = total
                else:
                    held[index] = total.astype(jnp.bfloat16)

            each(order, phase, body)

        pl.when(place == 0)(lambda: total_up((1,)))
        pl.when(place == extent - 1)(lambda: total_up((0,)))
        if extent > 2:
            pl.when((place > 0) & (place < extent - 1))(lambda: total_up((0, 1)))

    def drain(number, phase):
        axis = PARTS[number][2][phase]
        for way, goal in goals_of(axis):
            pl.when(runs(way, axis, goal)[0])(lambda: link(number, phase, way, goal).wait_send())

    core_sum(1)
    chain(1, 0)
    core_sum(2)
    chain(2, 0)
    core_sum(0)
    chain(0, 0)
    finish(1, 0)
    chain(1, 1)
    finish(2, 0)
    chain(2, 1)
    finish(0, 0)
    chain(0, 1)
    finish(1, 1)
    chain(1, 2)
    finish(0, 1)
    chain(0, 2)
    finish(2, 1)
    chain(2, 2)
    finish(0, 2)
    finish(1, 2)
    finish(2, 2)
    for number in range(3):
        for copy in core_copies[number]:
            copy.wait_send()
        for phase in range(3):
            drain(number, phase)


def spread_kernel(sizes, basis_ref, all_ref, core_send, core_recv, send_sem, recv_sem, own_sem):
    dims, here, core = where_am_i(sizes)
    own = pltpu.make_async_copy(basis_ref, all_ref.at[here["x"], core, here["z"], here["y"]], own_sem)
    own.start()
    greet(dims, here, core)
    own.wait()
    orders = [order[::-1] for _, _, order in PARTS]

    def link(number, phase, way, origin):
        start, rows, _ = PARTS[number]
        order = orders[number]
        axis = order[phase]
        slot = (number * 3 + phase) * 8 + way * 4 + origin
        to = here[axis] + 1 if way == 0 else here[axis] - 1
        rest = [a for a in AXES if a not in order[: phase + 1]]
        block = all_ref.at[view(here, rest, {axis: origin}, start, rows, core)]
        return pltpu.make_async_remote_copy(
            src_ref=block,
            dst_ref=block,
            send_sem=send_sem.at[slot],
            recv_sem=recv_sem.at[slot],
            device_id=device(dims, here, core, **{axis: to}),
            device_id_type=MESH,
        )

    def steps_of(number, phase):
        axis = orders[number][phase]
        place, extent = here[axis], dims[axis]
        for i in range(extent):
            yield i, 0, place - i, place - i >= 0, place < extent - 1
            yield i, 1, place + i, place + i <= extent - 1, place > 0

    def chain(number, phase):
        for i, way, origin, exists, sends in steps_of(number, phase):
            if i == 0:
                pl.when(sends)(lambda: link(number, phase, way, origin).start())
            else:

                @pl.when(exists)
                def _():
                    link(number, phase, way, origin).wait_recv()
                    pl.when(sends)(lambda: link(number, phase, way, origin).start())

    def begin(number, phase):
        for i, way, origin, exists, sends in steps_of(number, phase):
            if i == 0:
                pl.when(sends)(lambda: link(number, phase, way, origin).start())

    def relay(number, phase):
        for i, way, origin, exists, sends in steps_of(number, phase):
            if i > 0:

                @pl.when(exists)
                def _():
                    link(number, phase, way, origin).wait_recv()
                    pl.when(sends)(lambda: link(number, phase, way, origin).start())

    def swap(number):
        start, rows, _ = PARTS[number]
        for x in range(dims["x"]):
            block = all_ref.at[x, core, :, :, pl.ds(start, rows), :]
            yield pltpu.make_async_remote_copy(
                src_ref=block,
                dst_ref=block,
                send_sem=core_send.at[number * dims["x"] + x],
                recv_sem=core_recv.at[number * dims["x"] + x],
                device_id=device(dims, here, 1 - core),
                device_id_type=MESH,
            )

    for phase in range(3):
        for number in range(3):
            if phase == 0:
                begin(number, 0)
        for number in (0, 2, 1) if phase == 0 else (0, 1, 2):
            relay(number, phase)
            if phase < 2:
                begin(number, phase + 1)
            else:
                for copy in swap(number):
                    copy.start()
    for number in range(3):
        for copy in swap(number):
            copy.wait()
        for phase in range(3):
            for i, way, origin, exists, sends in steps_of(number, phase):
                pl.when(exists & sends)(lambda: link(number, phase, way, origin).wait_send())


def sketch_kernel(slots, index_ref, rank_ref, col_ref, *refs):
    u_refs, v_refs = refs[:slots], refs[slots : 2 * slots]
    weights_ref, test_ref, sketch_ref, part_ref = refs[2 * slots :]
    home = pl.program_id(0)
    test = test_ref[...]
    sketches = []
    for slot in range(slots):
        weight = weights_ref[pl.ds(col_ref[home * slots + slot], 1), :]
        weighted = (v_refs[slot][0].astype(jnp.float32) * weight).astype(jnp.bfloat16)
        sketch = jnp.dot(weighted, test, preferred_element_type=jnp.float32)
        live = lax.broadcasted_iota(jnp.int32, sketch.shape, 0) < rank_ref[home * slots + slot]
        sketch = jnp.where(live, sketch, 0.0).astype(jnp.bfloat16)
        sketch_ref[slot] = sketch
        sketches.append(sketch)
    left = jnp.concatenate([u[0] for u in u_refs], axis=0)
    part = lax.dot_general(
        jnp.concatenate(sketches, axis=0), left, (((0,), (0,)), ((), ())), preferred_element_type=jnp.float32
    )
    part_ref[0] = part.astype(jnp.bfloat16)


def couple_kernel(group, home_ref, slot_ref, u_ref, basis_ref, sketch_ref, out_ref):
    first = pl.program_id(0) * group
    for i in range(group):
        basis = basis_ref[home_ref[first + i]]
        projected = lax.dot_general(u_ref[i], basis, (((1,), (1,)), ((), ())), preferred_element_type=jnp.float32)
        out_ref[i] = lax.dot_general(
            projected.astype(jnp.bfloat16), sketch_ref[slot_ref[first + i]], (((0,), (0,)), ((), ())), preferred_element_type=jnp.float32
        )


def per_device(
    sizes,
    factor_u,
    factor_v,
    tile_ranks,
    tile_rows,
    tile_cols,
    cluster_home,
    quad_weights,
    test_matrix,
    near_sketch,
):
    tiles, rank_max, nodes = factor_u.shape
    columns = test_matrix.shape[1]
    clusters = cluster_home.shape[0]
    slots = max(2, (tiles + clusters - 1) // clusters)
    dims = grid_of(sizes)
    homes = jnp.sum(jnp.where(tile_rows == lax.broadcasted_iota(jnp.int32, (tiles, clusters), 1), cluster_home[None, :], 0), axis=1)
    order = lax.broadcasted_iota(jnp.int32, (tiles, tiles), 0)
    earlier = (homes[:, None] == homes[None, :]) & (lax.broadcasted_iota(jnp.int32, (tiles, tiles), 1) < order)
    places = homes * slots + jnp.sum(earlier.astype(jnp.int32), axis=1)
    taken = places[None, :] == lax.broadcasted_iota(jnp.int32, (clusters * slots, tiles), 0)
    pick = lambda values: jnp.sum(jnp.where(taken, values[None, :], 0), axis=1)
    index, ranks, cols = pick(jnp.arange(tiles, dtype=jnp.int32)), pick(tile_ranks), pick(tile_cols)

    def tile_spec(slot):
        return pl.BlockSpec((1, rank_max, nodes), lambda h, index, ranks, cols: (index[h * slots + slot], 0, 0))

    sketch, parts = pl.pallas_call(
        functools.partial(sketch_kernel, slots),
        grid_spec=pltpu.PrefetchScalarGridSpec(
            num_scalar_prefetch=3,
            grid=(clusters,),
            in_specs=[tile_spec(slot) for slot in range(slots)] * 2
            + [
                pl.BlockSpec(quad_weights.shape, lambda h, *_: (0, 0)),
                pl.BlockSpec(test_matrix.shape, lambda h, *_: (0, 0)),
            ],
            out_specs=[
                pl.BlockSpec((slots, rank_max, columns), lambda h, *_: (h, 0, 0)),
                pl.BlockSpec((1, columns, nodes), lambda h, *_: (h, 0, 0)),
            ],
        ),
        out_shape=[
            jax.ShapeDtypeStruct((clusters * slots, rank_max, columns), jnp.bfloat16),
            jax.ShapeDtypeStruct((clusters, columns, nodes), jnp.bfloat16),
        ],
        name="sketch",
    )(index, ranks, cols, *([factor_u] * slots), *([factor_v] * slots), quad_weights, test_matrix)

    shape = (dims["x"], 2, dims["z"], dims["y"], columns, nodes)
    boxes = []
    for _, rows, axes in PARTS:
        for phase in range(3):
            rest = [dims[axis] for axis in AXES if axis not in axes[: phase + 1]]
            boxes += [pltpu.VMEM((dims[axes[phase]], *rest, rows, nodes), jnp.bfloat16)] * 2
    swaps = len(PARTS) * dims["x"]
    sems = [pltpu.SemaphoreType.DMA((swaps,))] * 2 + [pltpu.SemaphoreType.DMA((len(PARTS) * 24,))] * 2
    far_part = pl.pallas_call(
        functools.partial(reduce_kernel, sizes),
        out_shape=jax.ShapeDtypeStruct((columns, nodes), jnp.float32),
        in_specs=[VMEM],
        out_specs=VMEM,
        scratch_shapes=[pltpu.VMEM((shape[0], *shape[2:]), jnp.bfloat16), *boxes, *sems],
        compiler_params=pltpu.CompilerParams(collective_id=0, has_side_effects=True, vmem_limit_bytes=62 << 20),
        name="reduce",
    )(parts.reshape(shape))

    sketched = near_sketch[0].astype(jnp.float32).T + far_part
    gram = lax.dot_general(
        sketched, sketched, (((1,), (1,)), ((), ())), precision=lax.Precision.HIGHEST, preferred_element_type=jnp.float32
    )
    lower = jnp.linalg.cholesky(gram)
    basis = lax.linalg.triangular_solve(lower, sketched, left_side=True, lower=True).astype(jnp.bfloat16)

    bases = pl.pallas_call(
        functools.partial(spread_kernel, sizes),
        out_shape=jax.ShapeDtypeStruct(shape, jnp.bfloat16),
        in_specs=[VMEM],
        out_specs=VMEM,
        scratch_shapes=[*sems, pltpu.SemaphoreType.DMA],
        compiler_params=pltpu.CompilerParams(collective_id=1, has_side_effects=True, vmem_limit_bytes=62 << 20),
        name="spread",
    )(basis).reshape(clusters, columns, nodes)

    group = 8
    return pl.pallas_call(
        functools.partial(couple_kernel, group),
        grid_spec=pltpu.PrefetchScalarGridSpec(
            num_scalar_prefetch=2,
            grid=(tiles // group,),
            in_specs=[
                pl.BlockSpec((group, rank_max, nodes), lambda g, *_: (g, 0, 0)),
                pl.BlockSpec(bases.shape, lambda g, *_: (0, 0, 0), pipeline_mode=pl.Buffered(1)),
                pl.BlockSpec(sketch.shape, lambda g, *_: (0, 0, 0), pipeline_mode=pl.Buffered(1)),
            ],
            out_specs=pl.BlockSpec((group, columns, columns), lambda g, *_: (g, 0, 0)),
        ),
        out_shape=jax.ShapeDtypeStruct((tiles, columns, columns), jnp.float32),
        compiler_params=pltpu.CompilerParams(vmem_limit_bytes=62 << 20),
        name="couple",
    )(homes, places, factor_u, bases, sketch)


def solution(mesh):
    placed = (
        P(("tile", "row"), None, None),
        P(("tile", "row"), None, None),
        P(("tile", "row")),
        P(("tile", "row"), None),
        P(("tile", "row")),
        P(),
        P(),
        P(),
        P(("tile", "row"), None, None),
    )
    sizes = (mesh.shape["tile"], mesh.shape["row"])
    return jax.shard_map(
        functools.partial(per_device, sizes),
        mesh=mesh,
        in_specs=placed,
        out_specs=P(("tile", "row"), None, None),
        check_vma=False,
    )
```

```python
import functools

import jax
import jax.numpy as jnp
from jax import lax
from jax.experimental import pallas as pl
from jax.experimental.pallas import tpu as pltpu
from jax.sharding import PartitionSpec as P

MESH = pl.DeviceIdType.MESH
DEPTH = 4
VMEM = pl.BlockSpec(memory_space=pltpu.VMEM)


def grid_of(sizes):
    return {"x": sizes[0] // 2, "z": DEPTH, "y": sizes[1] // DEPTH}


def where_am_i(sizes):
    dims = grid_of(sizes)
    tile, row = lax.axis_index("tile"), lax.axis_index("row")
    here = {"x": tile // 2, "z": row // dims["y"], "y": row % dims["y"]}
    return dims, here, tile % 2


def device(dims, here, core, **moved):
    at = dict(here, **moved)
    return (at["x"] * 2 + core, at["z"] * dims["y"] + at["y"])


def greet(dims, here, core):
    barrier = pltpu.get_barrier_semaphore()
    pl.semaphore_signal(barrier, inc=1, device_id=device(dims, here, 1 - core), device_id_type=MESH)
    for axis, extent in dims.items():
        place = here[axis]

        @pl.when(place > 0)
        def _():
            pl.semaphore_signal(barrier, inc=1, device_id=device(dims, here, core, **{axis: place - 1}), device_id_type=MESH)

        @pl.when(place < extent - 1)
        def _():
            pl.semaphore_signal(barrier, inc=1, device_id=device(dims, here, core, **{axis: place + 1}), device_id_type=MESH)

    heard = 1
    for axis, extent in dims.items():
        heard = heard + jnp.where(here[axis] > 0, 1, 0) + jnp.where(here[axis] < extent - 1, 1, 0)
    pl.semaphore_wait(barrier, heard)


PARTS = ((0, 48, ("z", "x", "y")), (48, 48, ("x", "y", "z")), (96, 32, ("y", "z", "x")))
AXES = ("x", "z", "y")


def view(here, done, fixed, start, rows, core=None):
    index = []
    for axis in AXES:
        if axis in fixed:
            index.append(fixed[axis])
        elif axis in done:
            index.append(here[axis])
        else:
            index.append(slice(None))
        if axis == "x" and core is not None:
            index.append(core)
    return tuple(index) + (pl.ds(start, rows), slice(None))


def reduce_kernel(sizes, part_ref, far_ref, held, *scratch):
    boxes, (core_send, core_recv, send_sem, recv_sem) = scratch[:-4], scratch[-4:]
    dims, here, core = where_am_i(sizes)
    greet(dims, here, core)
    sems = {}

    def sem_of(*key):
        return sems.setdefault(key, len(sems))

    box_of = {}
    for number, (_, _, order) in enumerate(PARTS):
        for phase in range(3):
            for way in range(2):
                box_of[number, phase, way] = boxes[len(box_of)]

    core_copies = {}
    for number, (start, rows, _) in enumerate(PARTS):
        copies = []
        for x in range(dims["x"]):
            slot = sem_of("core", number, x)
            copy = pltpu.make_async_remote_copy(
                src_ref=part_ref.at[x, 1 - core, :, :, pl.ds(start, rows), :],
                dst_ref=held.at[x, :, :, pl.ds(start, rows), :],
                send_sem=core_send.at[slot],
                recv_sem=core_recv.at[slot],
                device_id=device(dims, here, 1 - core),
                device_id_type=MESH,
            )
            copy.start()
            copies.append(copy)
        core_copies[number] = copies

    zs, ys = dims["z"], dims["y"]

    def core_sum(number):
        start, rows, _ = PARTS[number]
        for x, copy in enumerate(core_copies[number]):
            copy.wait_recv()

            def add(i, carry):
                z, y = i // ys, i % ys
                own = part_ref[x, core, z, y, pl.ds(start, rows), :].astype(jnp.float32)
                got = held[x, z, y, pl.ds(start, rows), :].astype(jnp.float32)
                held[x, z, y, pl.ds(start, rows), :] = (own + got).astype(jnp.bfloat16)
                return carry

            lax.fori_loop(0, zs * ys, add, 0)

    def rest_of(order, phase):
        left = [axis for axis in AXES if axis not in order[: phase + 1]]
        count = 1
        for axis in left:
            count *= dims[axis]
        return left, count

    def each(order, phase, body):
        left, count = rest_of(order, phase)

        def step(i, carry):
            at, rem = {}, i
            for axis in reversed(left):
                at[axis] = rem % dims[axis]
                rem = rem // dims[axis]
            body(at, tuple(at[axis] for axis in left))
            return carry

        if count == 1:
            step(0, 0)
        else:
            lax.fori_loop(0, count, step, 0)

    def link(number, phase, way, goal):
        start, rows, order = PARTS[number]
        axis = order[phase]
        slot = (number * 3 + phase) * 8 + way * 4 + goal
        to = here[axis] + 1 if way == 0 else here[axis] - 1
        return pltpu.make_async_remote_copy(
            src_ref=held.at[view(here, order[:phase], {axis: goal}, start, rows)],
            dst_ref=box_of[number, phase, way].at[goal],
            send_sem=send_sem.at[slot],
            recv_sem=recv_sem.at[slot],
            device_id=device(dims, here, core, **{axis: to}),
            device_id_type=MESH,
        )

    def runs(way, axis, goal):
        place, extent = here[axis], dims[axis]
        sends = place < goal if way == 0 else place > goal
        relays = place > 0 if way == 0 else place < extent - 1
        return sends, relays

    def goals_of(axis):
        extent = dims[axis]
        for i in range(1, extent):
            yield 0, extent - i
            yield 1, i - 1

    def begin(number, phase):
        axis = PARTS[number][2][phase]
        for way, goal in goals_of(axis):
            sends, relays = runs(way, axis, goal)
            pl.when(sends & ~relays)(lambda: link(number, phase, way, goal).start())

    def relay(number, phase):
        start, rows, order = PARTS[number]
        axis = order[phase]
        if dims[axis] == 2:
            return
        for way, goal in goals_of(axis):
            sends, relays = runs(way, axis, goal)

            @pl.when(sends & relays)
            def _():
                link(number, phase, way, goal).wait_recv()

                def body(at, rest):
                    index = view(here, order[:phase], dict(at, **{axis: goal}), start, rows)
                    total = held[index].astype(jnp.float32) + box_of[number, phase, way][(goal,) + rest].astype(jnp.float32)
                    held[index] = total.astype(jnp.bfloat16)

                each(order, phase, body)
                link(number, phase, way, goal).start()

    def finish(number, phase):
        start, rows, order = PARTS[number]
        axis = order[phase]
        place, extent = here[axis], dims[axis]

        def total_up(ways):
            for way in ways:
                link(number, phase, way, place).wait_recv()

            def body(at, rest):
                index = view(here, order[:phase], dict(at, **{axis: place}), start, rows)
                total = held[index].astype(jnp.float32)
                for way in ways:
                    total = total + box_of[number, phase, way][(place,) + rest].astype(jnp.float32)
                if phase == 2:
                    far_ref[pl.ds(start, rows), :] = total
                else:
                    held[index] = total.astype(jnp.bfloat16)

            each(order, phase, body)

        pl.when(place == 0)(lambda: total_up((1,)))
        pl.when(place == extent - 1)(lambda: total_up((0,)))
        if extent > 2:
            pl.when((place > 0) & (place < extent - 1))(lambda: total_up((0, 1)))

    def drain(number, phase):
        axis = PARTS[number][2][phase]
        for way, goal in goals_of(axis):
            pl.when(runs(way, axis, goal)[0])(lambda: link(number, phase, way, goal).wait_send())

    for number in range(3):
        core_sum(number)
        begin(number, 0)
    relay(0, 0)
    for phase in range(3):
        for number in (1, 2, 0):
            if (number, phase) != (0, 0):
                relay(number, phase)
        for number in (1, 2, 0):
            finish(number, phase)
            if phase < 2:
                begin(number, phase + 1)
    for number in range(3):
        for copy in core_copies[number]:
            copy.wait_send()
        for phase in range(3):
            drain(number, phase)


def spread_kernel(sizes, basis_ref, all_ref, core_send, core_recv, send_sem, recv_sem, own_sem):
    dims, here, core = where_am_i(sizes)
    own = pltpu.make_async_copy(basis_ref, all_ref.at[here["x"], core, here["z"], here["y"]], own_sem)
    own.start()
    greet(dims, here, core)
    own.wait()
    orders = [order[::-1] for _, _, order in PARTS]

    def link(number, phase, way, origin):
        start, rows, _ = PARTS[number]
        order = orders[number]
        axis = order[phase]
        slot = (number * 3 + phase) * 8 + way * 4 + origin
        to = here[axis] + 1 if way == 0 else here[axis] - 1
        rest = [a for a in AXES if a not in order[: phase + 1]]
        block = all_ref.at[view(here, rest, {axis: origin}, start, rows, core)]
        return pltpu.make_async_remote_copy(
            src_ref=block,
            dst_ref=block,
            send_sem=send_sem.at[slot],
            recv_sem=recv_sem.at[slot],
            device_id=device(dims, here, core, **{axis: to}),
            device_id_type=MESH,
        )

    def steps_of(number, phase):
        axis = orders[number][phase]
        place, extent = here[axis], dims[axis]
        for i in range(extent):
            yield i, 0, place - i, place - i >= 0, place < extent - 1
            yield i, 1, place + i, place + i <= extent - 1, place > 0

    def begin(number, phase):
        for i, way, origin, exists, sends in steps_of(number, phase):
            if i == 0:
                pl.when(sends)(lambda: link(number, phase, way, origin).start())

    def relay(number, phase):
        for i, way, origin, exists, sends in steps_of(number, phase):
            if i > 0:

                @pl.when(exists)
                def _():
                    link(number, phase, way, origin).wait_recv()
                    pl.when(sends)(lambda: link(number, phase, way, origin).start())
                    swap(number, phase, origin).start()

    def swap(number, phase, origin):
        start, rows, _ = PARTS[number]
        order = orders[number]
        rest = [a for a in AXES if a not in order[: phase + 1]]
        block = all_ref.at[view(here, rest, {order[phase]: origin}, start, rows, core)]
        slot = (number * 3 + phase) * 4 + origin
        return pltpu.make_async_remote_copy(
            src_ref=block,
            dst_ref=block,
            send_sem=core_send.at[slot],
            recv_sem=core_recv.at[slot],
            device_id=device(dims, here, 1 - core),
            device_id_type=MESH,
        )

    for number in range(3):
        begin(number, 0)
    for number in range(3):
        swap(number, 0, here[orders[number][0]]).start()
    for phase in range(3):
        for number in (0, 2, 1) if phase == 0 else (0, 1, 2):
            relay(number, phase)
            if phase < 2:
                begin(number, phase + 1)
    for number in range(3):
        swap(number, 0, here[orders[number][0]]).wait()
        for phase in range(3):
            for i, way, origin, exists, sends in steps_of(number, phase):
                pl.when(exists & sends)(lambda: link(number, phase, way, origin).wait_send())
                if i > 0:
                    pl.when(exists)(lambda: swap(number, phase, origin).wait())


def sketch_kernel(homes, slots, index_ref, rank_ref, col_ref, *refs):
    count = homes * slots
    u_refs, v_refs = refs[:count], refs[count : 2 * count]
    weights_ref, test_ref, sketch_ref, part_ref = refs[2 * count :]
    first = pl.program_id(0) * count
    test = test_ref[...]
    sketches = []
    for slot in range(count):
        weight = weights_ref[pl.ds(col_ref[first + slot], 1), :]
        weighted = (v_refs[slot][0].astype(jnp.float32) * weight).astype(jnp.bfloat16)
        sketch = jnp.dot(weighted, test, preferred_element_type=jnp.float32)
        live = lax.broadcasted_iota(jnp.int32, sketch.shape, 0) < rank_ref[first + slot]
        sketch = jnp.where(live, sketch, 0.0).astype(jnp.bfloat16)
        sketch_ref[slot] = sketch
        sketches.append(sketch)
    for home in range(homes):
        own = slice(home * slots, (home + 1) * slots)
        part = lax.dot_general(
            jnp.concatenate(sketches[own], axis=0),
            jnp.concatenate([u[0] for u in u_refs[own]], axis=0),
            (((0,), (0,)), ((), ())),
            preferred_element_type=jnp.float32,
        )
        part_ref[home] = part.astype(jnp.bfloat16)


def couple_kernel(group, home_ref, slot_ref, u_ref, basis_ref, sketch_ref, out_ref):
    first = pl.program_id(0) * group
    projected = [
        lax.dot_general(basis_ref[home_ref[first + i]], u_ref[i], (((1,), (1,)), ((), ())), preferred_element_type=jnp.float32).astype(jnp.bfloat16)
        for i in range(group)
    ]
    for i in range(group):
        out_ref[i] = jnp.dot(projected[i], sketch_ref[slot_ref[first + i]], preferred_element_type=jnp.float32)


def per_device(
    sizes,
    factor_u,
    factor_v,
    tile_ranks,
    tile_rows,
    tile_cols,
    cluster_home,
    quad_weights,
    test_matrix,
    near_sketch,
):
    tiles, rank_max, nodes = factor_u.shape
    columns = test_matrix.shape[1]
    clusters = cluster_home.shape[0]
    slots = max(2, (tiles + clusters - 1) // clusters)
    dims = grid_of(sizes)
    homes = jnp.sum(jnp.where(tile_rows == lax.broadcasted_iota(jnp.int32, (tiles, clusters), 1), cluster_home[None, :], 0), axis=1)
    order = lax.broadcasted_iota(jnp.int32, (tiles, tiles), 0)
    earlier = (homes[:, None] == homes[None, :]) & (lax.broadcasted_iota(jnp.int32, (tiles, tiles), 1) < order)
    places = homes * slots + jnp.sum(earlier.astype(jnp.int32), axis=1)
    taken = places[None, :] == lax.broadcasted_iota(jnp.int32, (clusters * slots, tiles), 0)
    pick = lambda values: jnp.sum(jnp.where(taken, values[None, :], 0), axis=1)
    index, ranks, cols = pick(jnp.arange(tiles, dtype=jnp.int32)), pick(tile_ranks), pick(tile_cols)

    batch = 4
    count = batch * slots

    def tile_spec(slot):
        return pl.BlockSpec((1, rank_max, nodes), lambda h, index, ranks, cols: (index[h * count + slot], 0, 0))

    sketch, parts = pl.pallas_call(
        functools.partial(sketch_kernel, batch, slots),
        grid_spec=pltpu.PrefetchScalarGridSpec(
            num_scalar_prefetch=3,
            grid=(clusters // batch,),
            in_specs=[tile_spec(slot) for slot in range(count)] * 2
            + [
                pl.BlockSpec(quad_weights.shape, lambda h, *_: (0, 0)),
                pl.BlockSpec(test_matrix.shape, lambda h, *_: (0, 0)),
            ],
            out_specs=[
                pl.BlockSpec((count, rank_max, columns), lambda h, *_: (h, 0, 0)),
                pl.BlockSpec((batch, columns, nodes), lambda h, *_: (h, 0, 0)),
            ],
        ),
        out_shape=[
            jax.ShapeDtypeStruct((clusters * slots, rank_max, columns), jnp.bfloat16),
            jax.ShapeDtypeStruct((clusters, columns, nodes), jnp.bfloat16),
        ],
        name="sketch",
    )(index, ranks, cols, *([factor_u] * count), *([factor_v] * count), quad_weights, test_matrix)

    shape = (dims["x"], 2, dims["z"], dims["y"], columns, nodes)
    boxes = []
    for _, rows, axes in PARTS:
        for phase in range(3):
            rest = [dims[axis] for axis in AXES if axis not in axes[: phase + 1]]
            boxes += [pltpu.VMEM((dims[axes[phase]], *rest, rows, nodes), jnp.bfloat16)] * 2
    swaps = len(PARTS) * 12
    sems = [pltpu.SemaphoreType.DMA((swaps,))] * 2 + [pltpu.SemaphoreType.DMA((len(PARTS) * 24,))] * 2
    far_part = pl.pallas_call(
        functools.partial(reduce_kernel, sizes),
        out_shape=jax.ShapeDtypeStruct((columns, nodes), jnp.float32),
        in_specs=[VMEM],
        out_specs=VMEM,
        scratch_shapes=[pltpu.VMEM((shape[0], *shape[2:]), jnp.bfloat16), *boxes, *sems],
        compiler_params=pltpu.CompilerParams(collective_id=0, has_side_effects=True, vmem_limit_bytes=62 << 20),
        name="reduce",
    )(parts.reshape(shape))

    sketched = near_sketch[0].astype(jnp.float32).T + far_part
    gram = lax.dot_general(
        sketched, sketched, (((1,), (1,)), ((), ())), precision=lax.Precision.HIGHEST, preferred_element_type=jnp.float32
    )
    lower = jnp.linalg.cholesky(gram)
    basis = lax.linalg.triangular_solve(lower, sketched, left_side=True, lower=True).astype(jnp.bfloat16)

    bases = pl.pallas_call(
        functools.partial(spread_kernel, sizes),
        out_shape=jax.ShapeDtypeStruct(shape, jnp.bfloat16),
        in_specs=[VMEM],
        out_specs=VMEM,
        scratch_shapes=[*sems, pltpu.SemaphoreType.DMA],
        compiler_params=pltpu.CompilerParams(collective_id=1, has_side_effects=True, vmem_limit_bytes=62 << 20),
        name="spread",
    )(basis).reshape(clusters, columns, nodes)

    group = 8
    return pl.pallas_call(
        functools.partial(couple_kernel, group),
        grid_spec=pltpu.PrefetchScalarGridSpec(
            num_scalar_prefetch=2,
            grid=(tiles // group,),
            in_specs=[
                pl.BlockSpec((group, rank_max, nodes), lambda g, *_: (g, 0, 0)),
                pl.BlockSpec(bases.shape, lambda g, *_: (0, 0, 0), pipeline_mode=pl.Buffered(1)),
                pl.BlockSpec(sketch.shape, lambda g, *_: (0, 0, 0), pipeline_mode=pl.Buffered(1)),
            ],
            out_specs=pl.BlockSpec((group, columns, columns), lambda g, *_: (g, 0, 0)),
        ),
        out_shape=jax.ShapeDtypeStruct((tiles, columns, columns), jnp.float32),
        compiler_params=pltpu.CompilerParams(vmem_limit_bytes=62 << 20),
        name="couple",
    )(homes, places, factor_u, bases, sketch)


def solution(mesh):
    placed = (
        P(("tile", "row"), None, None),
        P(("tile", "row"), None, None),
        P(("tile", "row")),
        P(("tile", "row"), None),
        P(("tile", "row")),
        P(),
        P(),
        P(),
        P(("tile", "row"), None, None),
    )
    sizes = (mesh.shape["tile"], mesh.shape["row"])
    return jax.shard_map(
        functools.partial(per_device, sizes),
        mesh=mesh,
        in_specs=placed,
        out_specs=P(("tile", "row"), None, None),
        check_vma=False,
    )
```

```python
import functools

import jax
import jax.numpy as jnp
from jax import lax
from jax.experimental import pallas as pl
from jax.experimental.pallas import tpu as pltpu
from jax.sharding import PartitionSpec as P

MESH = pl.DeviceIdType.MESH
DEPTH = 4
VMEM = pl.BlockSpec(memory_space=pltpu.VMEM)


def grid_of(sizes):
    return {"x": sizes[0] // 2, "z": DEPTH, "y": sizes[1] // DEPTH}


def where_am_i(sizes):
    dims = grid_of(sizes)
    tile, row = lax.axis_index("tile"), lax.axis_index("row")
    here = {"x": tile // 2, "z": row // dims["y"], "y": row % dims["y"]}
    return dims, here, tile % 2


def device(dims, here, core, **moved):
    at = dict(here, **moved)
    return (at["x"] * 2 + core, at["z"] * dims["y"] + at["y"])


def greet(dims, here, core):
    barrier = pltpu.get_barrier_semaphore()
    pl.semaphore_signal(barrier, inc=1, device_id=device(dims, here, 1 - core), device_id_type=MESH)
    for axis, extent in dims.items():
        place = here[axis]

        @pl.when(place > 0)
        def _():
            pl.semaphore_signal(barrier, inc=1, device_id=device(dims, here, core, **{axis: place - 1}), device_id_type=MESH)

        @pl.when(place < extent - 1)
        def _():
            pl.semaphore_signal(barrier, inc=1, device_id=device(dims, here, core, **{axis: place + 1}), device_id_type=MESH)

    heard = 1
    for axis, extent in dims.items():
        heard = heard + jnp.where(here[axis] > 0, 1, 0) + jnp.where(here[axis] < extent - 1, 1, 0)
    pl.semaphore_wait(barrier, heard)


PARTS = ((0, 48, ("z", "x", "y")), (48, 48, ("x", "y", "z")), (96, 32, ("y", "z", "x")))
AXES = ("x", "z", "y")


def view(here, done, fixed, start, rows, core=None):
    index = []
    for axis in AXES:
        if axis in fixed:
            index.append(fixed[axis])
        elif axis in done:
            index.append(here[axis])
        else:
            index.append(slice(None))
        if axis == "x" and core is not None:
            index.append(core)
    return tuple(index) + (pl.ds(start, rows), slice(None))


def reduce_kernel(sizes, part_ref, far_ref, held, *scratch):
    boxes, (core_send, core_recv, send_sem, recv_sem) = scratch[:-4], scratch[-4:]
    dims, here, core = where_am_i(sizes)
    greet(dims, here, core)
    sems = {}

    def sem_of(*key):
        return sems.setdefault(key, len(sems))

    box_of = {}
    for number, (_, _, order) in enumerate(PARTS):
        for phase in range(3):
            for way in range(2):
                box_of[number, phase, way] = boxes[len(box_of)]

    core_copies = {}
    for number, (start, rows, _) in enumerate(PARTS):
        copies = []
        for x in range(dims["x"]):
            slot = sem_of("core", number, x)
            copy = pltpu.make_async_remote_copy(
                src_ref=part_ref.at[x, 1 - core, :, :, pl.ds(start, rows), :],
                dst_ref=held.at[x, :, :, pl.ds(start, rows), :],
                send_sem=core_send.at[slot],
                recv_sem=core_recv.at[slot],
                device_id=device(dims, here, 1 - core),
                device_id_type=MESH,
            )
            copy.start()
            copies.append(copy)
        core_copies[number] = copies

    zs, ys = dims["z"], dims["y"]

    def core_sum(number):
        start, rows, _ = PARTS[number]
        for x, copy in enumerate(core_copies[number]):
            copy.wait_recv()

            def add(i, carry):
                z, y = i // ys, i % ys
                own = part_ref[x, core, z, y, pl.ds(start, rows), :].astype(jnp.float32)
                got = held[x, z, y, pl.ds(start, rows), :].astype(jnp.float32)
                held[x, z, y, pl.ds(start, rows), :] = (own + got).astype(jnp.bfloat16)
                return carry

            lax.fori_loop(0, zs * ys, add, 0)

    def rest_of(order, phase):
        left = [axis for axis in AXES if axis not in order[: phase + 1]]
        count = 1
        for axis in left:
            count *= dims[axis]
        return left, count

    def each(order, phase, body):
        left, count = rest_of(order, phase)

        def step(i, carry):
            at, rem = {}, i
            for axis in reversed(left):
                at[axis] = rem % dims[axis]
                rem = rem // dims[axis]
            body(at, tuple(at[axis] for axis in left))
            return carry

        if count == 1:
            step(0, 0)
        else:
            lax.fori_loop(0, count, step, 0)

    def link(number, phase, way, goal):
        start, rows, order = PARTS[number]
        axis = order[phase]
        slot = (number * 3 + phase) * 8 + way * 4 + goal
        to = here[axis] + 1 if way == 0 else here[axis] - 1
        return pltpu.make_async_remote_copy(
            src_ref=held.at[view(here, order[:phase], {axis: goal}, start, rows)],
            dst_ref=box_of[number, phase, way].at[goal],
            send_sem=send_sem.at[slot],
            recv_sem=recv_sem.at[slot],
            device_id=device(dims, here, core, **{axis: to}),
            device_id_type=MESH,
        )

    def runs(way, axis, goal):
        place, extent = here[axis], dims[axis]
        sends = place < goal if way == 0 else place > goal
        relays = place > 0 if way == 0 else place < extent - 1
        return sends, relays

    def goals_of(axis):
        extent = dims[axis]
        for i in range(1, extent):
            yield 0, extent - i
            yield 1, i - 1

    def begin(number, phase):
        axis = PARTS[number][2][phase]
        for way, goal in goals_of(axis):
            sends, relays = runs(way, axis, goal)
            pl.when(sends & ~relays)(lambda: link(number, phase, way, goal).start())

    def relay(number, phase):
        start, rows, order = PARTS[number]
        axis = order[phase]
        if dims[axis] == 2:
            return
        for way, goal in goals_of(axis):
            sends, relays = runs(way, axis, goal)

            @pl.when(sends & relays)
            def _():
                link(number, phase, way, goal).wait_recv()

                def body(at, rest):
                    index = view(here, order[:phase], dict(at, **{axis: goal}), start, rows)
                    total = held[index].astype(jnp.float32) + box_of[number, phase, way][(goal,) + rest].astype(jnp.float32)
                    held[index] = total.astype(jnp.bfloat16)

                each(order, phase, body)
                link(number, phase, way, goal).start()

    def finish(number, phase):
        start, rows, order = PARTS[number]
        axis = order[phase]
        place, extent = here[axis], dims[axis]

        def total_up(ways):
            for way in ways:
                link(number, phase, way, place).wait_recv()

            def body(at, rest):
                index = view(here, order[:phase], dict(at, **{axis: place}), start, rows)
                total = held[index].astype(jnp.float32)
                for way in ways:
                    total = total + box_of[number, phase, way][(place,) + rest].astype(jnp.float32)
                if phase == 2:
                    far_ref[pl.ds(start, rows), :] = total
                else:
                    held[index] = total.astype(jnp.bfloat16)

            each(order, phase, body)

        pl.when(place == 0)(lambda: total_up((1,)))
        pl.when(place == extent - 1)(lambda: total_up((0,)))
        if extent > 2:
            pl.when((place > 0) & (place < extent - 1))(lambda: total_up((0, 1)))

    def drain(number, phase):
        axis = PARTS[number][2][phase]
        for way, goal in goals_of(axis):
            pl.when(runs(way, axis, goal)[0])(lambda: link(number, phase, way, goal).wait_send())

    for number in range(3):
        core_sum(number)
        begin(number, 0)
    relay(0, 0)
    for phase in range(3):
        for number in (1, 2, 0):
            if (number, phase) != (0, 0):
                relay(number, phase)
        for number in (1, 2, 0):
            finish(number, phase)
            if phase < 2:
                begin(number, phase + 1)
    for number in range(3):
        for copy in core_copies[number]:
            copy.wait_send()
        for phase in range(3):
            drain(number, phase)


def spread_kernel(sizes, basis_ref, all_ref, core_send, core_recv, send_sem, recv_sem, own_sem):
    dims, here, core = where_am_i(sizes)
    own = pltpu.make_async_copy(basis_ref, all_ref.at[here["x"], core, here["z"], here["y"]], own_sem)
    own.start()
    greet(dims, here, core)
    own.wait()
    orders = [order[::-1] for _, _, order in PARTS]

    def link(number, phase, way, origin):
        start, rows, _ = PARTS[number]
        order = orders[number]
        axis = order[phase]
        slot = (number * 3 + phase) * 8 + way * 4 + origin
        to = here[axis] + 1 if way == 0 else here[axis] - 1
        rest = [a for a in AXES if a not in order[: phase + 1]]
        block = all_ref.at[view(here, rest, {axis: origin}, start, rows, core)]
        return pltpu.make_async_remote_copy(
            src_ref=block,
            dst_ref=block,
            send_sem=send_sem.at[slot],
            recv_sem=recv_sem.at[slot],
            device_id=device(dims, here, core, **{axis: to}),
            device_id_type=MESH,
        )

    def steps_of(number, phase):
        axis = orders[number][phase]
        place, extent = here[axis], dims[axis]
        for i in range(extent):
            yield i, 0, place - i, place - i >= 0, place < extent - 1
            yield i, 1, place + i, place + i <= extent - 1, place > 0

    def begin(number, phase):
        for i, way, origin, exists, sends in steps_of(number, phase):
            if i == 0:
                pl.when(sends)(lambda: link(number, phase, way, origin).start())

    def relay(number, phase):
        for i, way, origin, exists, sends in steps_of(number, phase):
            if i > 0:

                @pl.when(exists)
                def _():
                    link(number, phase, way, origin).wait_recv()
                    pl.when(sends)(lambda: link(number, phase, way, origin).start())
                    swap(number, phase, origin).start()

    def swap(number, phase, origin):
        start, rows, _ = PARTS[number]
        order = orders[number]
        rest = [a for a in AXES if a not in order[: phase + 1]]
        block = all_ref.at[view(here, rest, {order[phase]: origin}, start, rows, core)]
        slot = (number * 3 + phase) * 4 + origin
        return pltpu.make_async_remote_copy(
            src_ref=block,
            dst_ref=block,
            send_sem=core_send.at[slot],
            recv_sem=core_recv.at[slot],
            device_id=device(dims, here, 1 - core),
            device_id_type=MESH,
        )

    for number in range(3):
        begin(number, 0)
    for number in range(3):
        swap(number, 0, here[orders[number][0]]).start()
    for phase in range(3):
        for number in (0, 2, 1) if phase == 0 else (0, 1, 2):
            relay(number, phase)
            if phase < 2:
                begin(number, phase + 1)
    for number in range(3):
        swap(number, 0, here[orders[number][0]]).wait()
        for phase in range(3):
            for i, way, origin, exists, sends in steps_of(number, phase):
                pl.when(exists & sends)(lambda: link(number, phase, way, origin).wait_send())
                if i > 0:
                    pl.when(exists)(lambda: swap(number, phase, origin).wait())


def sketch_kernel(homes, slots, index_ref, rank_ref, col_ref, *refs):
    count = homes * slots
    u_refs, v_refs = refs[:count], refs[count : 2 * count]
    weights_ref, test_ref, sketch_ref, part_ref = refs[2 * count :]
    first = pl.program_id(0) * count
    test = test_ref[...]
    sketches = []
    for slot in range(count):
        weight = weights_ref[pl.ds(col_ref[first + slot], 1), :]
        weighted = (v_refs[slot][0].astype(jnp.float32) * weight).astype(jnp.bfloat16)
        sketch = jnp.dot(weighted, test, preferred_element_type=jnp.float32)
        live = lax.broadcasted_iota(jnp.int32, sketch.shape, 0) < rank_ref[first + slot]
        sketch = jnp.where(live, sketch, 0.0).astype(jnp.bfloat16)
        sketch_ref[slot] = sketch
        sketches.append(sketch)
    for home in range(homes):
        own = slice(home * slots, (home + 1) * slots)
        part = lax.dot_general(
            jnp.concatenate(sketches[own], axis=0),
            jnp.concatenate([u[0] for u in u_refs[own]], axis=0),
            (((0,), (0,)), ((), ())),
            preferred_element_type=jnp.float32,
        )
        part_ref[home] = part.astype(jnp.bfloat16)


BLOCK = 16


def basis_kernel(sketched_ref, basis_ref):
    sketched = sketched_ref[...]
    size = sketched.shape[0]
    gram = lax.dot_general(
        sketched, sketched, (((1,), (1,)), ((), ())), precision=lax.Precision.HIGHEST, preferred_element_type=jnp.float32
    )
    eye = lax.broadcasted_iota(jnp.int32, (size, size), 0) == lax.broadcasted_iota(jnp.int32, (size, size), 1)
    rest = jnp.concatenate([gram, eye.astype(jnp.float32)], axis=1)
    inverse = []
    row = lax.broadcasted_iota(jnp.int32, (BLOCK, 1), 0)
    for start in range(0, size, BLOCK):
        panel = rest[:BLOCK]
        for j in range(BLOCK):
            at = start + j
            factor = jnp.where(row > j, panel[:, at : at + 1] / panel[j : j + 1, at : at + 1], 0.0)
            panel = panel - factor * panel[j : j + 1]
        own = lax.broadcasted_iota(jnp.int32, (BLOCK, size), 1) == row + start
        pivots = jnp.sum(jnp.where(own, panel[:, :size], 0.0), axis=1, keepdims=True)
        inverse.append(panel[:, size:] * lax.rsqrt(pivots))
        if start + BLOCK < size:
            update = lax.dot_general(
                panel[:, :size] / pivots, panel, (((0,), (0,)), ((), ())), precision=lax.Precision.HIGHEST, preferred_element_type=jnp.float32
            )
            rest = rest[BLOCK:] - update[start + BLOCK :]
    basis_ref[...] = jnp.dot(
        jnp.concatenate(inverse, axis=0), sketched, precision=lax.Precision.HIGHEST, preferred_element_type=jnp.float32
    ).astype(jnp.bfloat16)


def couple_kernel(group, home_ref, slot_ref, u_ref, basis_ref, sketch_ref, out_ref):
    first = pl.program_id(0) * group
    projected = [
        lax.dot_general(basis_ref[home_ref[first + i]], u_ref[i], (((1,), (1,)), ((), ())), preferred_element_type=jnp.float32).astype(jnp.bfloat16)
        for i in range(group)
    ]
    for i in range(group):
        out_ref[i] = jnp.dot(projected[i], sketch_ref[slot_ref[first + i]], preferred_element_type=jnp.float32)


def per_device(
    sizes,
    factor_u,
    factor_v,
    tile_ranks,
    tile_rows,
    tile_cols,
    cluster_home,
    quad_weights,
    test_matrix,
    near_sketch,
):
    tiles, rank_max, nodes = factor_u.shape
    columns = test_matrix.shape[1]
    clusters = cluster_home.shape[0]
    slots = max(2, (tiles + clusters - 1) // clusters)
    dims = grid_of(sizes)
    homes = jnp.sum(jnp.where(tile_rows == lax.broadcasted_iota(jnp.int32, (tiles, clusters), 1), cluster_home[None, :], 0), axis=1)
    order = lax.broadcasted_iota(jnp.int32, (tiles, tiles), 0)
    earlier = (homes[:, None] == homes[None, :]) & (lax.broadcasted_iota(jnp.int32, (tiles, tiles), 1) < order)
    places = homes * slots + jnp.sum(earlier.astype(jnp.int32), axis=1)
    taken = places[None, :] == lax.broadcasted_iota(jnp.int32, (clusters * slots, tiles), 0)
    pick = lambda values: jnp.sum(jnp.where(taken, values[None, :], 0), axis=1)
    index, ranks, cols = pick(jnp.arange(tiles, dtype=jnp.int32)), pick(tile_ranks), pick(tile_cols)

    batch = 4
    count = batch * slots

    def tile_spec(slot):
        return pl.BlockSpec((1, rank_max, nodes), lambda h, index, ranks, cols: (index[h * count + slot], 0, 0))

    sketch, parts = pl.pallas_call(
        functools.partial(sketch_kernel, batch, slots),
        grid_spec=pltpu.PrefetchScalarGridSpec(
            num_scalar_prefetch=3,
            grid=(clusters // batch,),
            in_specs=[tile_spec(slot) for slot in range(count)] * 2
            + [
                pl.BlockSpec(quad_weights.shape, lambda h, *_: (0, 0)),
                pl.BlockSpec(test_matrix.shape, lambda h, *_: (0, 0)),
            ],
            out_specs=[
                pl.BlockSpec((count, rank_max, columns), lambda h, *_: (h, 0, 0)),
                pl.BlockSpec((batch, columns, nodes), lambda h, *_: (h, 0, 0)),
            ],
        ),
        out_shape=[
            jax.ShapeDtypeStruct((clusters * slots, rank_max, columns), jnp.bfloat16),
            jax.ShapeDtypeStruct((clusters, columns, nodes), jnp.bfloat16),
        ],
        name="sketch",
    )(index, ranks, cols, *([factor_u] * count), *([factor_v] * count), quad_weights, test_matrix)

    shape = (dims["x"], 2, dims["z"], dims["y"], columns, nodes)
    boxes = []
    for _, rows, axes in PARTS:
        for phase in range(3):
            rest = [dims[axis] for axis in AXES if axis not in axes[: phase + 1]]
            boxes += [pltpu.VMEM((dims[axes[phase]], *rest, rows, nodes), jnp.bfloat16)] * 2
    swaps = len(PARTS) * 12
    sems = [pltpu.SemaphoreType.DMA((swaps,))] * 2 + [pltpu.SemaphoreType.DMA((len(PARTS) * 24,))] * 2
    far_part = pl.pallas_call(
        functools.partial(reduce_kernel, sizes),
        out_shape=jax.ShapeDtypeStruct((columns, nodes), jnp.float32),
        in_specs=[VMEM],
        out_specs=VMEM,
        scratch_shapes=[pltpu.VMEM((shape[0], *shape[2:]), jnp.bfloat16), *boxes, *sems],
        compiler_params=pltpu.CompilerParams(collective_id=0, has_side_effects=True, vmem_limit_bytes=62 << 20),
        name="reduce",
    )(parts.reshape(shape))

    sketched = near_sketch[0].astype(jnp.float32).T + far_part
    basis = pl.pallas_call(
        basis_kernel,
        out_shape=jax.ShapeDtypeStruct((columns, nodes), jnp.bfloat16),
        in_specs=[VMEM],
        out_specs=VMEM,
        name="basis",
    )(sketched)

    bases = pl.pallas_call(
        functools.partial(spread_kernel, sizes),
        out_shape=jax.ShapeDtypeStruct(shape, jnp.bfloat16),
        in_specs=[VMEM],
        out_specs=VMEM,
        scratch_shapes=[*sems, pltpu.SemaphoreType.DMA],
        compiler_params=pltpu.CompilerParams(collective_id=1, has_side_effects=True, vmem_limit_bytes=62 << 20),
        name="spread",
    )(basis).reshape(clusters, columns, nodes)

    group = 16
    return pl.pallas_call(
        functools.partial(couple_kernel, group),
        grid_spec=pltpu.PrefetchScalarGridSpec(
            num_scalar_prefetch=2,
            grid=(tiles // group,),
            in_specs=[
                pl.BlockSpec((group, rank_max, nodes), lambda g, *_: (g, 0, 0)),
                pl.BlockSpec(bases.shape, lambda g, *_: (0, 0, 0), pipeline_mode=pl.Buffered(1)),
                pl.BlockSpec(sketch.shape, lambda g, *_: (0, 0, 0), pipeline_mode=pl.Buffered(1)),
            ],
            out_specs=pl.BlockSpec((group, columns, columns), lambda g, *_: (g, 0, 0)),
        ),
        out_shape=jax.ShapeDtypeStruct((tiles, columns, columns), jnp.float32),
        compiler_params=pltpu.CompilerParams(vmem_limit_bytes=62 << 20),
        name="couple",
    )(homes, places, factor_u, bases, sketch)


def solution(mesh):
    placed = (
        P(("tile", "row"), None, None),
        P(("tile", "row"), None, None),
        P(("tile", "row")),
        P(("tile", "row"), None),
        P(("tile", "row")),
        P(),
        P(),
        P(),
        P(("tile", "row"), None, None),
    )
    sizes = (mesh.shape["tile"], mesh.shape["row"])
    return jax.shard_map(
        functools.partial(per_device, sizes),
        mesh=mesh,
        in_specs=placed,
        out_specs=P(("tile", "row"), None, None),
        check_vma=False,
    )
```
